32 devices in a mesh: section: 4 (over y, core), expert: 4 (over z), mp: 2 (over x).
Axes of the slice: x: 2, y: 2, z: 4, core: 2. Of those that a mesh axis runs over, the one named last changes fastest.
Arguments:
- grad_top: bfloat16 [4, 64, 4096], P(None, 'expert', 'mp'), may hold values from -6 to 6
- w_down: bfloat16 [4, 4, 4096, 4096], P('section', 'expert', None, 'mp'), may hold values from -0.09375 to 0.09375
- w_up: bfloat16 [4, 4, 4096, 4096], P('section', 'expert', 'mp'), may hold values from -0.125 to 0.125
- saved: bfloat16 [4, 4, 4, 16, 4096], P('section', None, 'expert'), may hold values from -6 to 6
- assign: int32 [4, 4, 4, 4], P('section', None, 'expert'), may hold values from 0 to 3, as said below
- keep: int32 [4, 4], replicated, may hold values 0 or 1
Outputs:
- grads: bfloat16 [4, 4, 64, 4096], P('section', None, 'expert', 'mp')
The draws below stay inside these ranges and needn't reach their ends.
Inputs may be any that keep to these rules, and one draw needn't show every extreme that they name: Each row assign[l, m, i, :] names every expert exactly 1 times.
All inputs are finite; a program needn't handle non-finite values.
Results may differ from the reference program's by a relative error of at most 0.017.
Values may be sent and summed in bfloat16 or wider, within the bound.
A program may use at most 128 MiB of HBM per device.

```python
import jax
import jax.numpy as jnp
from jax import lax

D = 4096
FF = 4096
TILE = 4
PER = 1
MICRO = 4
SECTIONS = 4
EXPERTS = 4
GROUP = 1
FF_PART = 4096
TILES = 4
TOKENS = 64
ROWS_E = 16
N_EXPERT = 4


def draw_assign(key, part):
    count = SECTIONS * MICRO * N_EXPERT
    keys = jax.random.split(key, count)

    def draw_row(row_key):
        return jax.random.permutation(row_key, TILES)
    token_row_block = jax.vmap(draw_row)(keys)
    return (token_row_block // PER).reshape(SECTIONS, MICRO, N_EXPERT, TILES).astype(jnp.int32)


def plant(drawn, rng, low, high):
    longest = drawn.shape.index(max(drawn.shape))
    spots = []
    for shift in (0, 1):
        where = [jax.random.randint(jax.random.fold_in(rng, axis), (), 0, length) for axis, length in enumerate(drawn.shape)]
        where[longest] = (where[longest] + shift) % drawn.shape[longest]
        spots.append(tuple(where))
    return drawn.at[spots[0]].set(low).at[spots[1]].set(high)


def shard_levels(rng, shape, cuts, least, largest):
    loudness, own = 1.0, jax.random.fold_in(rng, 6)
    for axis_at, blocks in cuts:
        heights = jnp.exp(jax.random.uniform(jax.random.fold_in(own, axis_at), (blocks,), jnp.float32, least / len(cuts), largest / len(cuts)))
        loudness = loudness * jnp.repeat(heights, shape[axis_at] // blocks).reshape([-1 if axis == axis_at else 1 for axis in range(len(shape))])
    return loudness


def noise(stream_key, extent, deviation, bound, pieces=(), kind=jnp.bfloat16):
    loudness = shard_levels(stream_key, extent, pieces, -0.22, 0.18) if pieces else 1.0
    array = jax.random.normal(stream_key, extent, jnp.float32) * deviation * loudness
    return jnp.minimum(jnp.maximum(array, -bound), bound).astype(kind)


def setup_inputs(seed: int = 0) -> dict:
    key_list = jax.random.split(jax.random.key(seed), 7)
    grad_top = noise(key_list[0], (MICRO, TOKENS, D), 1.0, 6.0, ((1, 4), (2, 2)))
    w_down = noise(key_list[1], (SECTIONS, N_EXPERT, FF_PART, D), D ** -0.5, 0.09375, ((0, 4), (1, 4), (3, 2)))
    w_up = noise(key_list[2], (SECTIONS, N_EXPERT, D, FF_PART), (FF // 2) ** -0.5, 0.125, ((0, 4), (1, 4), (2, 2)))
    saved = noise(key_list[3], (SECTIONS, MICRO, N_EXPERT, ROWS_E, FF_PART), 1.0, 6.0, ((0, 4), (2, 4)))
    assign = draw_assign(jax.random.fold_in(key_list[6], 71), 0)
    keep = plant((jax.random.randint(key_list[5], (SECTIONS, MICRO), 0, 4) < 3).astype(jnp.int32), jax.random.fold_in(key_list[5], 1), 0, 1)
    return dict(grad_top=grad_top, w_down=w_down, w_up=w_up, saved=saved, assign=assign, keep=keep)


def apply_layer(current, down_all, up_all, stored, route_rows, factor):
    tiles = current.reshape(N_EXPERT, TILES, TILE, D)
    onehot = (route_rows[..., None] == jnp.arange(EXPERTS, dtype=jnp.int32)).astype(jnp.int32)
    before = jnp.cumsum(onehot, axis=1) - onehot
    tile_rank = jnp.sum(before * onehot, axis=-1).astype(jnp.int32)
    source = jnp.broadcast_to(jnp.arange(N_EXPERT, dtype=jnp.int32)[:, None], route_rows.shape)
    arrived = jnp.zeros((EXPERTS, N_EXPERT, PER, TILE, D), jnp.bfloat16).at[route_rows, source, tile_rank].set(tiles)

    def expert_step(expert_id):
        token_row_block = arrived[expert_id].reshape(ROWS_E, D)
        start = (expert_id * GROUP).astype(jnp.int32)
        down_weight_matrix = lax.dynamic_slice_in_dim(down_all, start, GROUP, 0)
        weights_up = lax.dynamic_slice_in_dim(up_all, start, GROUP, 0)
        pre_act = lax.dynamic_slice_in_dim(stored, start, GROUP, 0)
        hidden_state = jnp.einsum('ek,ytk->yet', token_row_block.astype(jnp.float32), down_weight_matrix.astype(jnp.float32))
        hidden_grad = jnp.where(pre_act > 0, hidden_state, 0.0).astype(jnp.bfloat16)
        parts = jnp.einsum('grf,gcf->grc', hidden_grad.astype(jnp.float32), weights_up.astype(jnp.float32)).astype(jnp.bfloat16)
        return jnp.sum(parts.astype(jnp.float32), axis=0)

    back_all = lax.map(expert_step, jnp.arange(EXPERTS, dtype=jnp.int32))
    back_all = back_all.reshape(EXPERTS, N_EXPERT, PER, TILE, D)
    row_updates = back_all[route_rows, source, tile_rank].reshape(TOKENS, D)
    return (current.astype(jnp.float32) + factor * row_updates).astype(jnp.bfloat16)


def reference(grad_top, w_down, w_up, saved, assign, keep):
    results = [[None for micro_index in range(MICRO)] for layer_index in range(SECTIONS)]
    for micro_index in range(MICRO):
        current = grad_top[micro_index]
        for layer_index in reversed(range(SECTIONS)):
            factor = keep[layer_index, micro_index].astype(jnp.float32)
            current = apply_layer(current, w_down[layer_index], w_up[layer_index], saved[layer_index, micro_index], assign[layer_index, micro_index], factor)
            results[layer_index][micro_index] = current
    return jnp.stack([jnp.stack(row_list) for row_list in results])
```

```python
import functools

import jax
import jax.numpy as jnp
from jax import lax
from jax.experimental import pallas as pl
from jax.experimental.pallas import tpu as pltpu
from jax.sharding import PartitionSpec as P

PER = 1
MESH = pl.DeviceIdType.MESH
NT = (((1,), (1,)), ((), ()))
CHUNKS = 4


def window_kernel(
    n_section, n_expert,
    top_ref, down_hbm, up_hbm, saved_ref, place_ref, back_ref, out_ref,
    down, up, cur, incoming, send_a, recv_a, send_b, recv_b, mp_send, mp_recv,
    rows, gathered, own, hidden,
    w_sem, a_send, a_recv, b_send, b_recv, m_send, m_recv, s_send, s_recv,
):
    s = lax.axis_index("section")
    e = lax.axis_index("expert")
    x = lax.axis_index("mp")
    micro = top_ref.shape[0]
    slab = send_a.shape[2]
    ff = down.shape[0]
    width = up.shape[0]
    fc, wc = ff // CHUNKS, width // CHUNKS
    down_copy = pltpu.make_async_copy(down_hbm, down, w_sem.at[0])
    up_copy = pltpu.make_async_copy(up_hbm, up, w_sem.at[1])
    down_copy.start()
    up_copy.start()

    barrier = pltpu.get_barrier_semaphore()
    for d in range(1, n_expert):
        pl.semaphore_signal(
            barrier, inc=1, device_id={"expert": lax.rem(e + d, n_expert)}, device_id_type=MESH
        )
    pl.semaphore_signal(barrier, inc=1, device_id={"mp": 1 - x}, device_id_type=MESH)
    for d in (1, n_section - 1):
        pl.semaphore_signal(
            barrier, inc=1, device_id={"section": lax.rem(s + d, n_section)}, device_id_type=MESH
        )
    pl.semaphore_wait(barrier, n_expert + 2)

    def tile_copy(m, d, src, dst, send_sem, recv_sem):
        peer = lax.rem(e + d, n_expert)
        return pltpu.make_async_remote_copy(
            src_ref=src.at[m, peer],
            dst_ref=dst.at[m, e],
            send_sem=send_sem.at[m, d],
            recv_sem=recv_sem.at[m, e],
            device_id={"expert": peer},
            device_id_type=MESH,
        )

    def tile_arrival(m, d, src, dst, send_sem, recv_sem):
        peer = lax.rem(e + d, n_expert)
        return pltpu.make_async_remote_copy(
            src_ref=src.at[m, peer],
            dst_ref=dst.at[m, peer],
            send_sem=send_sem.at[m, d],
            recv_sem=recv_sem.at[m, peer],
            device_id={"expert": peer},
            device_id_type=MESH,
        )

    def exchange(m, src, dst, send_sem, recv_sem):
        for k in range(n_expert):
            src[m, k] = rows[k * slab : (k + 1) * slab, :].astype(jnp.bfloat16)
        for d in range(1, n_expert):
            tile_copy(m, d, src, dst, send_sem, recv_sem).start()
        dst[m, e] = src[m, e]
        for d in range(1, n_expert):
            tile_arrival(m, d, src, dst, send_sem, recv_sem).wait_recv()
        for k in range(n_expert):
            gathered[k * slab : (k + 1) * slab, :] = dst[m, k].astype(jnp.float32)
        return gathered[...].astype(jnp.bfloat16)

    def mp_copy(m, c):
        return pltpu.make_async_remote_copy(
            src_ref=mp_send.at[m, c],
            dst_ref=mp_recv.at[m, c],
            send_sem=m_send.at[m, c],
            recv_sem=m_recv.at[m, c],
            device_id={"mp": 1 - x},
            device_id_type=MESH,
        )

    def section_copy(m):
        return pltpu.make_async_remote_copy(
            src_ref=out_ref.at[m],
            dst_ref=incoming.at[m],
            send_sem=s_send.at[m],
            recv_sem=s_recv.at[m],
            device_id={"section": lax.rem(s + n_section - 1, n_section)},
            device_id_type=MESH,
        )

    def step(m, carry):
        @pl.when(s == n_section - 1)
        def _():
            cur[...] = top_ref[m]

        @pl.when(s < n_section - 1)
        def _():
            section_copy(m).wait_recv()
            cur[...] = incoming[m]

        rows[...] = jnp.dot(place_ref[m], cur[...], preferred_element_type=jnp.float32)
        arrived = exchange(m, send_a, recv_a, a_send, a_recv)

        @pl.when(m == 0)
        def _():
            down_copy.wait()

        for c in range(CHUNKS):
            part = lax.dot_general(
                arrived, down[c * fc : (c + 1) * fc, :], NT, preferred_element_type=jnp.float32
            )
            own[:, c * fc : (c + 1) * fc] = part
            mp_send[m, c] = part.astype(jnp.bfloat16)
            mp_copy(m, c).start()
        for c in range(CHUNKS):
            mp_copy(m, c).wait_recv()
            total = own[:, c * fc : (c + 1) * fc] + mp_recv[m, c].astype(jnp.float32)
            gate = saved_ref[m, :, c * fc : (c + 1) * fc].astype(jnp.float32)
            hidden[:, c * fc : (c + 1) * fc] = jnp.where(gate > 0, total, 0.0).astype(jnp.bfloat16)

        @pl.when(m == 0)
        def _():
            up_copy.wait()

        for c in range(CHUNKS):
            rows[:, c * wc : (c + 1) * wc] = lax.dot_general(
                hidden[...], up[c * wc : (c + 1) * wc, :], NT, preferred_element_type=jnp.float32
            )
        returned = exchange(m, send_b, recv_b, b_send, b_recv)
        update = jnp.dot(back_ref[m], returned, preferred_element_type=jnp.float32)
        out_ref[m] = (cur[...].astype(jnp.float32) + update).astype(jnp.bfloat16)

        @pl.when(s > 0)
        def _():
            section_copy(m).start()

        for d in range(1, n_expert):
            tile_copy(m, d, send_a, recv_a, a_send, a_recv).wait_send()
            tile_copy(m, d, send_b, recv_b, b_send, b_recv).wait_send()
        for c in range(CHUNKS):
            mp_copy(m, c).wait_send()
        return carry

    lax.fori_loop(0, micro, step, 0)

    @pl.when(s > 0)
    def _():
        for m in range(micro):
            section_copy(m).wait_send()


def fused(grad_top, w_down, w_up, saved, assign, keep):
    n_section = lax.axis_size("section")
    n_expert = lax.axis_size("expert")
    micro, tokens, width = grad_top.shape
    ff = w_down.shape[2]
    tiles = assign.shape[-1]
    tile_rows = tokens // tiles
    slab = PER * tile_rows
    routes = assign[0, :, 0]
    factor = lax.dynamic_index_in_dim(keep, lax.axis_index("section"), 0, keepdims=False)
    spot = jnp.repeat(routes, tile_rows, axis=1) * tile_rows + jnp.arange(tokens, dtype=jnp.int32) % tile_rows
    ids = jnp.arange(tokens, dtype=jnp.int32)
    place = (spot[:, None, :] == ids[None, :, None]).astype(jnp.bfloat16)
    back = ((spot[:, :, None] == ids[None, None, :]) & (factor[:, None, None] > 0)).astype(jnp.bfloat16)
    bf, f32, dma = jnp.bfloat16, jnp.float32, pltpu.SemaphoreType.DMA
    vm = pl.BlockSpec(memory_space=pltpu.VMEM)
    hbm = pl.BlockSpec(memory_space=pl.ANY)
    out = pl.pallas_call(
        functools.partial(window_kernel, n_section, n_expert),
        out_shape=jax.ShapeDtypeStruct((micro, tokens, width), bf),
        in_specs=[vm, hbm, hbm, vm, vm, vm],
        out_specs=vm,
        scratch_shapes=[
            pltpu.VMEM((ff, width), bf),
            pltpu.VMEM((width, ff), bf),
            pltpu.VMEM((tokens, width), bf),
            pltpu.VMEM((micro, tokens, width), bf),
            pltpu.VMEM((micro, n_expert, slab, width), bf),
            pltpu.VMEM((micro, n_expert, slab, width), bf),
            pltpu.VMEM((micro, n_expert, slab, width), bf),
            pltpu.VMEM((micro, n_expert, slab, width), bf),
            pltpu.VMEM((micro, CHUNKS, tokens, ff // CHUNKS), bf),
            pltpu.VMEM((micro, CHUNKS, tokens, ff // CHUNKS), bf),
            pltpu.VMEM((tokens, width), f32),
            pltpu.VMEM((tokens, width), f32),
            pltpu.VMEM((tokens, ff), f32),
            pltpu.VMEM((tokens, ff), bf),
            dma((2,)),
            dma((micro, n_expert)),
            dma((micro, n_expert)),
            dma((micro, n_expert)),
            dma((micro, n_expert)),
            dma((micro, CHUNKS)),
            dma((micro, CHUNKS)),
            dma((micro,)),
            dma((micro,)),
        ],
        compiler_params=pltpu.CompilerParams(
            collective_id=0, has_side_effects=True, vmem_limit_bytes=60 * 1024 * 1024
        ),
    )(grad_top, w_down[0, 0], w_up[0, 0], saved[0, :, 0], place, back)
    return out[None]


def shifted(value, axis, by):
    peers = lax.axis_size(axis)
    pairs = [(i, i + by) for i in range(peers) if 0 <= i + by < peers]
    return lax.ppermute(value, axis, pairs)


def body(grad_top, w_down, w_up, saved, assign, keep):
    n_section = lax.axis_size("section")
    n_expert = lax.axis_size("expert")
    section_index = lax.axis_index("section")
    tiles_dev = assign.shape[-1]
    experts = tiles_dev // PER
    group_size = n_expert // experts
    micro_count = grad_top.shape[0]
    token_rows = grad_top.shape[1]
    width = grad_top.shape[2]
    tile_rows = token_rows // tiles_dev
    slab_rows = PER * tile_rows
    down_projection = w_down[0, 0]
    up_proj = w_up[0, 0]
    stored = saved[0, :, 0]
    routes = assign[0, :, 0]
    rows_e = stored.shape[1]
    results = jnp.zeros((micro_count, token_rows, width), jnp.bfloat16)
    incoming = jnp.zeros((token_rows, width), jnp.bfloat16)
    steps_total = micro_count + n_section - 1
    for turn in range(steps_total):
        raw_index = turn - (n_section - 1) + section_index
        active = (raw_index >= 0) & (raw_index < micro_count)
        micro_index = jnp.clip(raw_index, 0, micro_count - 1)
        top_grad = lax.dynamic_index_in_dim(grad_top, micro_index, 0, keepdims=False)
        current = jnp.where(section_index == n_section - 1, top_grad, incoming)
        route_row = lax.dynamic_index_in_dim(routes, micro_index, 0, keepdims=False)
        onehot = (route_row[:, None] == jnp.arange(experts, dtype=jnp.int32)[None, :]).astype(
            jnp.int32
        )
        before = jnp.cumsum(onehot, axis=0) - onehot
        tile_rank = jnp.sum(before * onehot, axis=1)
        position_index = route_row * PER + tile_rank
        placing = (
            position_index[None, :] == jnp.arange(tiles_dev, dtype=jnp.int32)[:, None]
        ).astype(jnp.bfloat16)
        ordered = jnp.dot(
            placing,
            current.reshape(tiles_dev, tile_rows * width),
            preferred_element_type=jnp.float32,
        ).astype(jnp.bfloat16)
        outgoing = jnp.broadcast_to(
            ordered.reshape(experts, 1, slab_rows, width), (experts, group_size, slab_rows, width)
        )
        outgoing = outgoing.reshape(n_expert, slab_rows, width)
        arrived = lax.all_to_all(
            outgoing, "expert", split_axis=0, concat_axis=0, tiled=True
        ).reshape(rows_e, width)
        partial_value = lax.dot_general(
            arrived, down_projection, (((1,), (1,)), ((), ())), preferred_element_type=jnp.float32
        )
        pre_act = lax.dynamic_index_in_dim(stored, micro_index, 0, keepdims=False)
        expert_share_total = lax.psum_scatter(
            partial_value.astype(jnp.bfloat16), "mp", scatter_dimension=0, tiled=True
        ).astype(jnp.float32)
        share_rows = rows_e // lax.axis_size("mp")
        own_rows = lax.dynamic_slice_in_dim(
            pre_act, lax.axis_index("mp") * share_rows, share_rows, 0
        )
        local_grad = jnp.where(own_rows > 0, expert_share_total, 0.0).astype(jnp.bfloat16)
        hidden_grad = lax.all_gather(local_grad, "mp", axis=0, tiled=True)
        back_part = lax.dot_general(
            hidden_grad, up_proj, (((1,), (1,)), ((), ())), preferred_element_type=jnp.float32
        ).astype(jnp.bfloat16)
        returned = lax.all_to_all(
            back_part.reshape(n_expert, slab_rows, width),
            "expert",
            split_axis=0,
            concat_axis=0,
            tiled=True,
        )
        summed = jnp.sum(
            returned.reshape(experts, group_size, slab_rows, width), axis=1, dtype=jnp.float32
        )
        row_updates = jnp.take(summed, position_index, axis=0).reshape(token_rows, width)
        factor = keep[section_index, micro_index].astype(jnp.float32)
        fresh_grad = (current.astype(jnp.float32) + factor * row_updates).astype(jnp.bfloat16)
        previous = lax.dynamic_index_in_dim(results, micro_index, 0, keepdims=False)
        results = lax.dynamic_update_index_in_dim(
            results, jnp.where(active, fresh_grad, previous), micro_index, 0
        )
        if turn + 1 < steps_total:
            incoming = shifted(fresh_grad, "section", -1)
    return results[None]


def solution(mesh):
    placed = (
        P(None, "expert", "mp"),
        P("section", "expert", None, "mp"),
        P("section", "expert", "mp", None),
        P("section", None, "expert", None, None),
        P("section", None, "expert", None),
        P(),
    )
    whole_experts = mesh.shape["expert"] == 4 and mesh.shape["mp"] == 2 and mesh.shape["section"] == 4

    def choose(grad_top, w_down, w_up, saved, assign, keep):
        one_each = assign.shape[-1] == mesh.shape["expert"] and PER == 1
        form = fused if whole_experts and one_each else body
        return form(grad_top, w_down, w_up, saved, assign, keep)

    return jax.shard_map(
        choose,
        mesh=mesh,
        in_specs=placed,
        out_specs=P("section", None, "expert", "mp"),
        check_vma=False,
    )
```
